32 devices in a mesh: ctx: 16 (over z, x, core), head: 2 (over y).
Axes of the slice: x: 2, y: 2, z: 4, core: 2. Of those that a mesh axis runs over, the one named last changes fastest.
Arguments:
- keys: bfloat16 [8192, 1024], P('ctx', 'head'), may hold values from -6 to 6
- values: bfloat16 [8192, 1024], P('ctx', 'head'), may hold values from -6 to 6
- rates: float32 [2, 8192], P('head', 'ctx'), may hold values from 0.05 to 1
- queries: bfloat16 [8192, 1024], P(('ctx', 'head')), may hold values from -6 to 6
- fast_weights: bfloat16 [2, 3, 512, 512], P('head'), may hold values from -4 to 4
- gate: bfloat16 [8192, 1024], P(('ctx', 'head')), may hold values from -6 to 6
- gain: float32 [1024], replicated, may hold values from 0.1 to 1.9
Outputs:
- layer_out: bfloat16 [8192, 1024], P(('ctx', 'head'))
- new_weights: bfloat16 [2, 3, 512, 512], P('head')
The draws below stay inside these ranges and needn't reach their ends.
All inputs are finite; a program needn't handle non-finite values.
Results may differ from the reference program's by a relative error of at most 0.023.
Values may be sent and summed in bfloat16 or wider, within the bound.
No kernel may reach another device: no remote copies, remote signals or barrier semaphores. Data moves between devices by JAX's collectives and lax.ppermute only.
A program may use at most 64 MiB of HBM per device.

```python
import math
import jax
import jax.numpy as jnp
from jax import lax

DH = 512
NS_STEPS = 5
HEADS = 2
D = 1024
TOKENS = 8192


def level_of(rng, dims, cuts, smallest, top_value):
    def one(axis_at, blocks):
        steps = jax.random.uniform(jax.random.fold_in(jax.random.fold_in(rng, 6), axis_at), (blocks,), jnp.float32, smallest / len(cuts), top_value / len(cuts))
        return jnp.repeat(jnp.exp(steps), dims[axis_at] // blocks).reshape((-1,) + (1,) * (len(dims) - axis_at - 1))

    level = one(*cuts[0])
    for cut in cuts[1:]:
        level = level * one(*cut)
    return level


def normal_values(stream_key, shape, deviation, limit, shards=(), held_as=jnp.bfloat16):
    values = deviation * jax.random.normal(stream_key, shape, jnp.float32)
    if shards:
        values = values * level_of(stream_key, shape, shards, -0.22, 0.18)
    return jnp.clip(values, -limit, limit).astype(held_as)


def setup_inputs(seed: int = 0) -> dict:
    streams_of = jax.random.split(jax.random.key(seed), 8)
    return {
        "keys": normal_values(streams_of[0], (TOKENS, D), 1.0, 6.0, ((0, 16), (1, 2))),
        "values": normal_values(streams_of[1], (TOKENS, D), 1.0, 6.0, ((0, 16), (1, 2))),
        "rates": jnp.clip(jnp.exp(math.log(1.0) - 2.9957323 * jax.random.uniform(streams_of[2], (HEADS, TOKENS), jnp.float32) ** level_of(streams_of[2], (HEADS, TOKENS), ((0, 2), (1, 16)), -0.2, 0.2)), 0.05, 1.0),
        "queries": normal_values(streams_of[3], (TOKENS, D), 1.0, 6.0, ((0, 32),)),
        "fast_weights": normal_values(streams_of[4], (HEADS, 3, DH, DH), 1.0, 4.0, ((0, 2),)),
        "gate": normal_values(streams_of[5], (TOKENS, D), 1.0, 6.0, ((0, 32),)),
        "gain": jnp.clip(1.0 + 0.18 * jax.random.normal(streams_of[6], (D,), jnp.float32), 0.1, 1.9),
    }


coef_a = 3.4445
coef_b = -4.775
coef_c = 2.0315

def mat(left, right):
    return jnp.dot(left, right, preferred_element_type=jnp.float32)

def orthogonalize(grad):
    total = jnp.sum(grad * grad)
    iterate = (grad / (jnp.sqrt(total) + 1e-07)).astype(jnp.bfloat16)
    for step in range(NS_STEPS):
        gram = mat(iterate, iterate.T).astype(jnp.bfloat16)
        square = mat(gram, gram)
        poly = (coef_b * gram.astype(jnp.float32) + coef_c * square).astype(jnp.bfloat16)
        iterate = (coef_a * iterate.astype(jnp.float32) + mat(poly, iterate)).astype(jnp.bfloat16)
    return iterate

def head_terms(items):
    key_h, value_h, rate_h, query_h, weight_h = items
    scale = DH ** (-0.5)
    g_one = mat(key_h, weight_h[0]) * scale
    g_three = mat(key_h, weight_h[1]) * scale
    sig = jax.nn.sigmoid(g_one)
    hidden = (g_one * sig * g_three).astype(jnp.bfloat16)
    grad_out = (-(rate_h[:, None] * value_h.astype(jnp.float32))).astype(jnp.bfloat16)
    d_two = mat(hidden.T, grad_out) * scale
    d_hidden = mat(grad_out, weight_h[2].T) * scale
    dg_one = (d_hidden * g_three * sig * (1.0 + g_one * (1.0 - sig))).astype(jnp.bfloat16)
    dg_three = (d_hidden * (g_one * sig)).astype(jnp.bfloat16)
    d_one = mat(key_h.T, dg_one) * scale
    d_three = mat(key_h.T, dg_three) * scale
    grads = [d_one, d_three, d_two]
    updated = []
    for index in range(3):
        direction = orthogonalize(grads[index])
        updated.append((weight_h[index].astype(jnp.float32) - 0.4 * jnp.sqrt(jnp.float32(DH)) * direction.astype(jnp.float32)).astype(jnp.bfloat16))
    new_head = jnp.stack(updated)
    r_one = mat(query_h, weight_h[0]) * scale
    r_three = mat(query_h, weight_h[1]) * scale
    hq = (jax.nn.silu(r_one) * r_three).astype(jnp.bfloat16)
    read = (mat(hq, weight_h[2]) * scale).astype(jnp.bfloat16)
    return (read, new_head)

def reference(keys, values, rates, queries, fast_weights, gate, gain):
    tokens = keys.shape[0]
    heads = fast_weights.shape[0]

    def split(array):
        return array.reshape(tokens, heads, DH).transpose(1, 0, 2)
    read, new_weights = lax.map(head_terms, (split(keys), split(values), rates, split(queries), fast_weights))
    read32 = read.transpose(1, 0, 2).astype(jnp.float32)
    mean_sq = lax.optimization_barrier(jnp.mean(read32 * read32, axis=-1, keepdims=True))
    gate32 = gate.astype(jnp.float32).reshape(tokens, heads, DH)
    normed = read32 * lax.rsqrt(mean_sq + 1e-06) * gain.reshape(heads, DH) * jax.nn.silu(gate32)
    return (normed.reshape(tokens, heads * DH).astype(jnp.bfloat16), new_weights)
```

```python
import functools
import math

import jax
import jax.numpy as jnp
from jax import lax
from jax.experimental import pallas as pl
from jax.experimental.pallas import tpu as pltpu
from jax.sharding import PartitionSpec as P

NS_STEPS = 5
coef_a = 3.4445
coef_b = -4.775
coef_c = 2.0315
BF = jnp.bfloat16
F32 = jnp.float32
MIB = 1 << 20
ANY = pl.BlockSpec(memory_space=pl.ANY)
VM = pl.BlockSpec(memory_space=pltpu.VMEM)


def dot(left, right):
    return jnp.dot(left, right, preferred_element_type=F32)


def dot_nt(left, right):
    return lax.dot_general(left, right, (((1,), (1,)), ((), ())), preferred_element_type=F32)


def dot_tn(left, right):
    return lax.dot_general(left, right, (((0,), (0,)), ((), ())), preferred_element_type=F32)


def copies(pairs, sems):
    made = [pltpu.make_async_copy(src, dst, sems.at[i]) for i, (src, dst) in enumerate(pairs)]
    for copy in made:
        copy.start()
    return made


def quarter_id():
    return lax.axis_index("ctx") & 3


def put_pieces(whole, pieces):
    rows = whole.shape[0] // 4
    own = quarter_id()
    for r, piece in enumerate(pieces):
        at = pl.multiple_of((own ^ r) * rows, rows)
        piece[...] = whole[pl.ds(at, rows), :]


def take_pieces(pieces, whole):
    rows = whole.shape[0] // 4
    own = quarter_id()
    for r, piece in enumerate(pieces):
        at = pl.multiple_of((own ^ r) * rows, rows)
        whole[pl.ds(at, rows), :] = piece[...]


def grad_two_kernel(k_hbm, v_hbm, r_ref, w_hbm, *refs):
    pieces, (g1_ref, g3_ref, go_ref), (k, v, w1, w3, whole, sems) = refs[:4], refs[4:7], refs[7:]
    ck, c1, c3, cv = copies(
        [(k_hbm, k), (w_hbm.at[0, 0], w1), (w_hbm.at[0, 1], w3), (v_hbm, v)], sems
    )
    scale = w1.shape[-1] ** (-0.5)
    ck.wait()
    c1.wait()
    g1 = dot(k[...], w1[...]) * scale
    g1_ref[...] = g1
    c3.wait()
    g3 = dot(k[...], w3[...]) * scale
    g3_ref[...] = g3
    cv.wait()
    rate = jnp.broadcast_to(r_ref[...], (128, r_ref.shape[1])).T[:, :1]
    go = (-(rate * v[...].astype(F32))).astype(BF)
    go_ref[...] = go
    hidden = (g1 * jax.nn.sigmoid(g1) * g3).astype(BF)
    whole[...] = (dot_tn(hidden, go) * scale).astype(BF)
    put_pieces(whole, pieces)


def grad_one_kernel(k_ref, w_hbm, g1_ref, g3_ref, go_ref, *refs):
    one, three, (w2, dg1, dg3, whole, sems) = refs[:4], refs[4:8], refs[8:]
    (c2,) = copies([(w_hbm.at[0, 2], w2)], sems)
    scale = w2.shape[-1] ** (-0.5)
    c2.wait()
    dh = dot_nt(go_ref[...], w2[...]) * scale
    g1 = g1_ref[...]
    sig = jax.nn.sigmoid(g1)
    dg1[...] = (dh * g3_ref[...] * sig * (1.0 + g1 * (1.0 - sig))).astype(BF)
    dg3[...] = (dh * (g1 * sig)).astype(BF)
    k = k_ref[...]
    whole[...] = (dot_tn(k, dg1[...]) * scale).astype(BF)
    put_pieces(whole, one)
    whole[...] = (dot_tn(k, dg3[...]) * scale).astype(BF)
    put_pieces(whole, three)


def orthogonalize(grad):
    grad = grad.astype(F32)
    total = jnp.sum(grad * grad)
    x = (grad / (jnp.sqrt(total) + 1e-07)).astype(BF)
    for _ in range(NS_STEPS):
        gram = dot_nt(x, x).astype(BF)
        square = dot(gram, gram)
        poly = (coef_b * gram.astype(F32) + coef_c * square).astype(BF)
        x = (coef_a * x.astype(F32) + dot(poly, x)).astype(BF)
    return x


def updated(weight, x):
    step_size = 0.4 * math.sqrt(x.shape[-1])
    return (weight.astype(F32) - step_size * x.astype(F32)).astype(BF)


def first_update_kernel(p0, p2, p1, p3, w_hbm, o_ref, w, whole, sems):
    index = 2 * (1 - (lax.axis_index("ctx") & 1))
    (cw,) = copies([(w_hbm.at[0, index], w)], sems)
    take_pieces((p0, p1, p2, p3), whole)
    x = orthogonalize(whole[...])
    cw.wait()
    o_ref[...] = updated(w[...], x)


def last_update_kernel(p0, p1, p2, p3, w_hbm, mine, theirs, o_hbm, w, new, whole, sems):
    index = 2 * (1 - (lax.axis_index("ctx") & 1))
    cw, cm, ct = copies(
        [(w_hbm.at[0, 1], w), (mine, o_hbm.at[0, index]), (theirs, o_hbm.at[0, 2 - index])], sems
    )
    take_pieces((p0, p1, p2, p3), whole)
    x = orthogonalize(whole[...])
    cw.wait()
    new[...] = updated(w[...], x)
    cn = pltpu.make_async_copy(new, o_hbm.at[0, 1], sems.at[3])
    cn.start()
    cm.wait()
    ct.wait()
    cn.wait()


def read_kernel(w_hbm, *refs):
    count = (len(refs) - 4) // 2
    queries, reads, (w1, w3, w2, sems) = refs[:count], refs[count : 2 * count], refs[2 * count :]
    made = copies([(w_hbm.at[0, 0], w1), (w_hbm.at[0, 1], w3), (w_hbm.at[0, 2], w2)], sems)
    scale = w1.shape[-1] ** (-0.5)
    for copy in made:
        copy.wait()
    for q, out in zip(queries, reads):
        rows = q[...]
        r1 = dot(rows, w1[...]) * scale
        r3 = dot(rows, w3[...]) * scale
        hq = (r1 * jax.nn.sigmoid(r1) * r3).astype(BF)
        out[...] = (dot(hq, w2[...]) * scale).astype(BF)


def norm_kernel(heads, gate, gain, *refs):
    reads, out = refs[:heads], refs[heads]
    width = reads[0].shape[-1]
    me = lax.axis_index("head")
    for r, read in enumerate(reads):
        at = pl.multiple_of(lax.rem(me + r, heads) * width, width)
        x = read[...].astype(F32)
        mean = jnp.mean(x * x, axis=-1, keepdims=True)
        g = gate[:, pl.ds(at, width)].astype(F32)
        out[:, pl.ds(at, width)] = (
            x * lax.rsqrt(mean + 1e-06) * gain[:, pl.ds(at, width)] * (g * jax.nn.sigmoid(g))
        ).astype(BF)


def params(mib):
    return pltpu.CompilerParams(vmem_limit_bytes=mib * MIB)


def local(ctx, heads, keys, values, rates, queries, fast_weights, gate, gain):
    tok, width = keys.shape
    rows = width // 4
    piece = jax.ShapeDtypeStruct((rows, width), BF)
    bits = [1 << b for b in range(ctx.bit_length() - 1)]

    def swap(x, bit):
        return lax.ppermute(x, "ctx", [(i, i ^ bit) for i in range(ctx)])

    def turn(x, r):
        return lax.ppermute(x, "head", [(i, (i + r) % heads) for i in range(heads)])

    me = lax.axis_index("head")
    core = lax.axis_index("ctx") & 1

    def columns(r):
        return lax.dynamic_slice_in_dim(queries, lax.rem(me + r, heads) * width, width, 1)

    asked = [columns(0)] + [turn(columns(r), r) for r in range(1, heads)]

    mat = lambda dtype: pltpu.VMEM((width, width), dtype)
    tokens = lambda dtype: pltpu.VMEM((tok, width), dtype)
    outs = pl.pallas_call(
        grad_two_kernel,
        out_shape=[piece] * 4
        + [jax.ShapeDtypeStruct((tok, width), d) for d in (F32, F32, BF)],
        in_specs=[ANY, ANY, VM, ANY],
        out_specs=[VM] * 7,
        scratch_shapes=[tokens(BF), tokens(BF), mat(BF), mat(BF), mat(BF), pltpu.SemaphoreType.DMA((4,))],
        compiler_params=params(24),
    )(keys, values, rates, fast_weights)
    two, (g1, g3, go) = outs[:4], outs[4:]
    outs = pl.pallas_call(
        grad_one_kernel,
        out_shape=[piece] * 8,
        in_specs=[VM, ANY, VM, VM, VM],
        out_specs=[VM] * 8,
        scratch_shapes=[mat(BF), tokens(BF), tokens(BF), mat(BF), pltpu.SemaphoreType.DMA((1,))],
        compiler_params=params(24),
    )(keys, fast_weights, g1, g3, go)
    one, three = outs[:4], outs[4:]

    def add(x, y):
        return (x.astype(F32) + y.astype(F32)).astype(BF)

    def summed(p):
        far = swap(p[3], 1)
        near = swap(p[1], 1)
        give = add(p[2], far)
        keep = add(p[0], near)
        total = add(keep, swap(give, 2))
        for bit in bits[2:]:
            total = add(total, swap(total, bit))
        return total, swap(total, 2)

    two, one, three = summed(two), summed(one), summed(three)

    give = [jnp.where(core == 0, o, t) for o, t in zip(one, two)]
    keep = [jnp.where(core == 0, t, o) for o, t in zip(one, two)]
    got = [swap(x, 1) for x in give]
    matrix = jax.ShapeDtypeStruct((width, width), BF)
    mine = pl.pallas_call(
        first_update_kernel,
        out_shape=matrix,
        in_specs=[VM] * 4 + [ANY],
        out_specs=VM,
        scratch_shapes=[mat(BF), mat(BF), pltpu.SemaphoreType.DMA((1,))],
        compiler_params=params(16),
    )(*keep, *got, fast_weights)
    theirs = swap(mine, 1)
    others = [swap(x, 1) for x in three]
    new_weights = pl.pallas_call(
        last_update_kernel,
        out_shape=jax.ShapeDtypeStruct(fast_weights.shape, BF),
        in_specs=[VM] * 4 + [ANY] * 3,
        out_specs=ANY,
        scratch_shapes=[mat(BF), mat(BF), mat(BF), pltpu.SemaphoreType.DMA((4,))],
        compiler_params=params(16),
    )(three[0], others[0], three[1], others[1], fast_weights, mine, theirs)

    reads = pl.pallas_call(
        read_kernel,
        out_shape=[jax.ShapeDtypeStruct(x.shape, BF) for x in asked],
        in_specs=[ANY] + [VM] * heads,
        out_specs=[VM] * heads,
        scratch_shapes=[mat(BF)] * 3 + [pltpu.SemaphoreType.DMA((3,))],
        compiler_params=params(24),
    )(fast_weights, *asked)
    back = [reads[0]] + [turn(reads[r], heads - r) for r in range(1, heads)]
    layer_out = pl.pallas_call(
        functools.partial(norm_kernel, heads),
        out_shape=jax.ShapeDtypeStruct(queries.shape, BF),
        in_specs=[VM] * (2 + heads),
        out_specs=VM,
        compiler_params=params(16),
    )(gate, gain.reshape(1, -1), *back)
    return layer_out, new_weights


def solution(mesh):
    in_specs = (
        P("ctx", "head"),
        P("ctx", "head"),
        P("head", "ctx"),
        P(("ctx", "head"), None),
        P("head", None, None, None),
        P(("ctx", "head"), None),
        P(),
    )
    out_specs = (P(("ctx", "head"), None), P("head", None, None, None))
    body = functools.partial(local, mesh.shape["ctx"], mesh.shape["head"])
    return jax.shard_map(body, mesh=mesh, in_specs=in_specs, out_specs=out_specs, check_vma=False)
```

```python
import functools
import math

import jax
import jax.numpy as jnp
from jax import lax
from jax.experimental import pallas as pl
from jax.experimental.pallas import tpu as pltpu
from jax.sharding import PartitionSpec as P


NS_STEPS = 5
coef_a = 3.4445
coef_b = -4.775
coef_c = 2.0315
PLANS = {'A': (0, 1, 2), 'B': (0, 2), 'C': (0, 1)}
BF = jnp.bfloat16
F32 = jnp.float32
MIB = 1 << 20
ANY = pl.BlockSpec(memory_space=pl.ANY)
HBM = pl.BlockSpec(memory_space=pltpu.HBM)
VM = pl.BlockSpec(memory_space=pltpu.VMEM)


def dot(left, right):
    return jnp.dot(left, right, preferred_element_type=F32)


def dot_nt(left, right):
    return lax.dot_general(left, right, (((1,), (1,)), ((), ())), preferred_element_type=F32)


def dot_tn(left, right):
    return lax.dot_general(left, right, (((0,), (0,)), ((), ())), preferred_element_type=F32)


def copies(pairs, sems):
    made = [pltpu.make_async_copy(src, dst, sems.at[i]) for i, (src, dst) in enumerate(pairs)]
    for copy in made:
        copy.start()
    return made


def blocks(whole, bits):
    index = lax.axis_index("ctx")
    own = sum(((index >> b) & 1) << i for i, b in enumerate(bits))
    parts = 1 << (len(bits) - 2)
    rows = whole.shape[0] // (4 * parts)
    for r in range(4):
        for e in range(parts):
            at = pl.multiple_of((own ^ (r | (e << 2))) * rows, rows)
            yield r, pl.ds(e * rows, rows), pl.ds(at, rows)


def put_pieces(whole, pieces, bits):
    for r, part, rows in blocks(whole, bits):
        pieces[r][part, :] = whole[rows, :]


def take_pieces(pieces, whole, bits):
    for r, part, rows in blocks(whole, bits):
        whole[rows, :] = pieces[r][part, :]


def grad_two_kernel(heads, k_hbm, v_hbm, r_hbm, w_hbm, q_hbm, *refs):
    pieces, (g1_ref, g3_ref, go_ref), asked = refs[:4], refs[4:7], refs[7 : 7 + heads]
    k, v, r_ref, w1, w3, whole, sems = refs[7 + heads :]
    width = w1.shape[-1]
    me = lax.axis_index("head")
    columns = []
    for r, out in enumerate(asked):
        at = pl.multiple_of(lax.rem(me + r, heads) * width, width)
        columns.append((q_hbm.at[:, pl.ds(at, width)], out))
    ck, c1, c3, cv, cr, *cq = copies(
        [(k_hbm, k), (w_hbm.at[0, 0], w1), (w_hbm.at[0, 1], w3), (v_hbm, v), (r_hbm, r_ref)]
        + columns,
        sems,
    )
    scale = w1.shape[-1] ** (-0.5)
    ck.wait()
    c1.wait()
    g1 = dot(k[...], w1[...]) * scale
    g1_ref[...] = g1
    c3.wait()
    g3 = dot(k[...], w3[...]) * scale
    g3_ref[...] = g3
    cv.wait()
    cr.wait()
    rate = jnp.broadcast_to(r_ref[...], (128, r_ref.shape[1])).T[:, :1]
    go = (-(rate * v[...].astype(F32))).astype(BF)
    go_ref[...] = go
    hidden = (g1 * jax.nn.sigmoid(g1) * g3).astype(BF)
    whole[...] = (dot_tn(hidden, go) * scale).astype(BF)
    put_pieces(whole, pieces, PLANS["A"])
    for copy in cq:
        copy.wait()


def grad_one_kernel(k_hbm, w_hbm, g1_ref, g3_ref, go_ref, *refs):
    one, three, (w2, k, dg1, dg3, whole, sems) = refs[:4], refs[4:8], refs[8:]
    c2, ck = copies([(w_hbm.at[0, 2], w2), (k_hbm, k)], sems)
    scale = w2.shape[-1] ** (-0.5)
    c2.wait()
    dh = dot_nt(go_ref[...], w2[...]) * scale
    g1 = g1_ref[...]
    sig = jax.nn.sigmoid(g1)
    dg1[...] = (dh * g3_ref[...] * sig * (1.0 + g1 * (1.0 - sig))).astype(BF)
    dg3[...] = (dh * (g1 * sig)).astype(BF)
    ck.wait()
    whole[...] = (dot_tn(k[...], dg1[...]) * scale).astype(BF)
    put_pieces(whole, one, PLANS["B"])
    whole[...] = (dot_tn(k[...], dg3[...]) * scale).astype(BF)
    put_pieces(whole, three, PLANS["C"])


def orthogonalize(grad):
    grad = grad.astype(F32)
    total = jnp.sum(grad * grad)
    x = (grad / (jnp.sqrt(total) + 1e-07)).astype(BF)
    for _ in range(NS_STEPS):
        gram = dot_nt(x, x).astype(BF)
        square = dot(gram, gram)
        poly = (coef_b * gram.astype(F32) + coef_c * square).astype(BF)
        x = (coef_a * x.astype(F32) + dot(poly, x)).astype(BF)
    return x


def updated(weight, x):
    step_size = 0.4 * math.sqrt(x.shape[-1])
    return (weight.astype(F32) - step_size * x.astype(F32)).astype(BF)


def first_update_kernel(p0, p2, p1, p3, w_hbm, o_ref, w, whole, sems):
    index = 2 * (1 - (lax.axis_index("ctx") & 1))
    (cw,) = copies([(w_hbm.at[0, index], w)], sems)
    pieces = (p0, p1, p2, p3)

    @pl.when(index == 2)
    def _():
        take_pieces(pieces, whole, PLANS["A"])

    @pl.when(index == 0)
    def _():
        take_pieces(pieces, whole, PLANS["B"])

    x = orthogonalize(whole[...])
    cw.wait()
    o_ref[...] = updated(w[...], x)


def last_update_kernel(p0, p1, p2, p3, w_hbm, mine, theirs, o_hbm, w, new, whole, sems):
    index = 2 * (1 - (lax.axis_index("ctx") & 1))
    cw, cm, ct = copies(
        [(w_hbm.at[0, 1], w), (mine, o_hbm.at[0, index]), (theirs, o_hbm.at[0, 2 - index])], sems
    )
    take_pieces((p0, p1, p2, p3), whole, PLANS["C"])
    x = orthogonalize(whole[...])
    cw.wait()
    new[...] = updated(w[...], x)
    cn = pltpu.make_async_copy(new, o_hbm.at[0, 1], sems.at[3])
    cn.start()
    cm.wait()
    ct.wait()
    cn.wait()


def read_kernel(w_hbm, *refs):
    count = (len(refs) - 4) // 2
    queries, reads, (w1, w3, w2, sems) = refs[:count], refs[count : 2 * count], refs[2 * count :]
    made = copies([(w_hbm.at[0, 0], w1), (w_hbm.at[0, 1], w3), (w_hbm.at[0, 2], w2)], sems)
    scale = w1.shape[-1] ** (-0.5)
    for copy in made:
        copy.wait()
    for q, out in zip(queries, reads):
        rows = q[...]
        r1 = dot(rows, w1[...]) * scale
        r3 = dot(rows, w3[...]) * scale
        hq = (r1 * jax.nn.sigmoid(r1) * r3).astype(BF)
        out[...] = (dot(hq, w2[...]) * scale).astype(BF)


def norm_kernel(heads, gate, gain, *refs):
    reads, out = refs[:heads], refs[heads]
    width = reads[0].shape[-1]
    me = lax.axis_index("head")
    for r, read in enumerate(reads):
        at = pl.multiple_of(lax.rem(me + r, heads) * width, width)
        x = read[...].astype(F32)
        mean = jnp.mean(x * x, axis=-1, keepdims=True)
        g = gate[:, pl.ds(at, width)].astype(F32)
        out[:, pl.ds(at, width)] = (
            x * lax.rsqrt(mean + 1e-06) * gain[:, pl.ds(at, width)] * (g * jax.nn.sigmoid(g))
        ).astype(BF)


def local(ctx, heads, keys, values, rates, queries, fast_weights, gate, gain):
    tok, width = keys.shape
    bits = range(ctx.bit_length() - 1)
    core = lax.axis_index("ctx") & 1
    piece = jax.ShapeDtypeStruct((width // 4, width), BF)
    matrix = jax.ShapeDtypeStruct((width, width), BF)
    mat = lambda dtype: pltpu.VMEM((width, width), dtype)
    tokens = lambda dtype: pltpu.VMEM((tok, width), dtype)
    sems = lambda n: pltpu.SemaphoreType.DMA((n,))

    hbm = lambda x: pltpu.with_memory_space_constraint(x, pltpu.HBM)

    def call(kernel, mib, **kw):
        def run(*args):
            return pl.pallas_call(
                kernel, compiler_params=pltpu.CompilerParams(vmem_limit_bytes=mib * MIB), **kw
            )(*args)

        return run

    def swap(x, bit):
        return lax.ppermute(x, "ctx", [(i, i ^ (1 << bit)) for i in range(ctx)])

    def turn(x, r):
        return lax.ppermute(x, "head", [(i, (i + r) % heads) for i in range(heads)])

    outs = call(
        functools.partial(grad_two_kernel, heads), 14,
        out_shape=[piece] * 4
        + [jax.ShapeDtypeStruct((tok, width), d) for d in (F32, F32, BF)]
        + [jax.ShapeDtypeStruct((queries.shape[0], width), BF)] * heads,
        in_specs=[HBM] * 5,
        out_specs=[VM] * (7 + heads),
        scratch_shapes=[
            tokens(BF), tokens(BF), pltpu.VMEM(rates.shape, F32), mat(BF), mat(BF), mat(BF), sems(5 + heads)
        ],
    )(hbm(keys), hbm(values), hbm(rates), hbm(fast_weights), hbm(queries))
    two, (g1, g3, go), columns = outs[:4], outs[4:7], outs[7:]
    asked = [columns[0]] + [turn(columns[r], r) for r in range(1, heads)]
    outs = call(
        grad_one_kernel, 12,
        out_shape=[piece] * 8,
        in_specs=[HBM, HBM, VM, VM, VM],
        out_specs=[VM] * 8,
        scratch_shapes=[mat(BF), tokens(BF), tokens(BF), tokens(BF), mat(BF), sems(2)],
    )(hbm(keys), hbm(fast_weights), g1, g3, go)
    one, three = outs[:4], outs[4:]

    def add(x, y):
        return (x.astype(F32) + y.astype(F32)).astype(BF)

    def summed(n, p):
        plan = PLANS[n]
        far = swap(p[3], 0)
        near = swap(p[1], 0)
        give = add(p[2], far)
        keep = add(p[0], near)
        total = add(keep, swap(give, plan[1]))
        if len(plan) == 3:
            half = total.shape[0] // 2
            total = add(total[:half], swap(total[half:], plan[2]))
        for bit in bits:
            if bit not in plan:
                total = add(total, swap(total, bit))
        if len(plan) == 3:
            total = jnp.concatenate([total, swap(total, plan[2])])
        return total, swap(total, plan[1])

    two, one, three = summed("A", two), summed("B", one), summed("C", three)

    give = [jnp.where(core == 0, o, t) for o, t in zip(one, two)]
    keep = [jnp.where(core == 0, t, o) for o, t in zip(one, two)]
    got = [swap(x, 0) for x in give]
    mine = call(
        first_update_kernel, 10,
        out_shape=matrix,
        in_specs=[VM] * 4 + [HBM],
        out_specs=VM,
        scratch_shapes=[mat(BF), mat(BF), sems(1)],
    )(*keep, *got, hbm(fast_weights))
    theirs = swap(mine, 0)
    others = [swap(x, 0) for x in three]
    new_weights = call(
        last_update_kernel, 10,
        out_shape=jax.ShapeDtypeStruct(fast_weights.shape, BF),
        in_specs=[VM] * 4 + [HBM, ANY, ANY],
        out_specs=HBM,
        scratch_shapes=[mat(BF), mat(BF), mat(BF), sems(4)],
    )(three[0], others[0], three[1], others[1], hbm(fast_weights), mine, theirs)

    reads = call(
        read_kernel, 12,
        out_shape=[jax.ShapeDtypeStruct(x.shape, BF) for x in asked],
        in_specs=[HBM] + [VM] * heads,
        out_specs=[VM] * heads,
        scratch_shapes=[mat(BF)] * 3 + [sems(3)],
    )(hbm(fast_weights), *asked)
    back = [reads[0]] + [turn(reads[r], heads - r) for r in range(1, heads)]
    layer_out = call(
        functools.partial(norm_kernel, heads), 8,
        out_shape=jax.ShapeDtypeStruct(queries.shape, BF),
        in_specs=[VM] * (2 + heads),
        out_specs=VM,
    )(gate, gain.reshape(1, -1), *back)
    return layer_out, new_weights


def solution(mesh):
    in_specs = (
        P("ctx", "head"),
        P("ctx", "head"),
        P("head", "ctx"),
        P(("ctx", "head"), None),
        P("head", None, None, None),
        P(("ctx", "head"), None),
        P(),
    )
    out_specs = (P(("ctx", "head"), None), P("head", None, None, None))

    def body(*args):
        return local(mesh.shape["ctx"], mesh.shape["head"], *args)

    return jax.shard_map(
        body, mesh=mesh, in_specs=in_specs, out_specs=out_specs, check_vma=False
    )
```

```python
import functools
import math

import jax
import jax.numpy as jnp
from jax import lax
from jax.experimental import pallas as pl
from jax.experimental.pallas import tpu as pltpu
from jax.sharding import PartitionSpec as P


NS_STEPS = 5
coef_a = 3.4445
coef_b = -4.775
coef_c = 2.0315
PLANS = {'A': (0, 1, 2), 'B': (0, 2, 1), 'C': (0, 1)}
BF = jnp.bfloat16
F32 = jnp.float32
MIB = 1 << 20
ANY = pl.BlockSpec(memory_space=pl.ANY)
HBM = pl.BlockSpec(memory_space=pltpu.HBM)
VM = pl.BlockSpec(memory_space=pltpu.VMEM)


def dot(left, right):
    return jnp.dot(left, right, preferred_element_type=F32)


def dot_nt(left, right):
    return lax.dot_general(left, right, (((1,), (1,)), ((), ())), preferred_element_type=F32)


def dot_tn(left, right):
    return lax.dot_general(left, right, (((0,), (0,)), ((), ())), preferred_element_type=F32)


def copies(pairs, sems):
    made = [pltpu.make_async_copy(src, dst, sems.at[i]) for i, (src, dst) in enumerate(pairs)]
    for copy in made:
        copy.start()
    return made


def blocks(whole, bits):
    index = lax.axis_index("ctx")
    own = sum(((index >> b) & 1) << i for i, b in enumerate(bits))
    parts = 1 << (len(bits) - 2)
    rows = whole.shape[0] // (4 * parts)
    for r in range(4):
        for e in range(parts):
            at = pl.multiple_of((own ^ (r | (e << 2))) * rows, rows)
            yield r, pl.ds(e * rows, rows), pl.ds(at, rows)


def put_pieces(whole, pieces, bits):
    for r, part, rows in blocks(whole, bits):
        pieces[r][part, :] = whole[rows, :]


def take_pieces(pieces, whole, bits):
    for r, part, rows in blocks(whole, bits):
        whole[rows, :] = pieces[r][part, :]


def grad_two_kernel(heads, k_hbm, v_hbm, r_hbm, w_hbm, q_hbm, *refs):
    pieces, (g1_ref, g3_ref, go_ref), (k, w1, w3, w2) = refs[:4], refs[4:7], refs[7:11]
    asked = refs[11 : 11 + heads]
    v, r_ref, whole, sems = refs[11 + heads :]
    width = w1.shape[-1]
    me = lax.axis_index("head")
    columns = []
    for r, out in enumerate(asked):
        at = pl.multiple_of(lax.rem(me + r, heads) * width, width)
        columns.append((q_hbm.at[:, pl.ds(at, width)], out))
    ck, c1, c3, cv, cr, *cq = copies(
        [(k_hbm, k), (w_hbm.at[0, 0], w1), (w_hbm.at[0, 1], w3), (v_hbm, v), (r_hbm, r_ref)]
        + [(w_hbm.at[0, 2], w2)]
        + columns,
        sems,
    )
    scale = w1.shape[-1] ** (-0.5)
    ck.wait()
    c1.wait()
    g1 = dot(k[...], w1[...]) * scale
    g1_ref[...] = g1
    c3.wait()
    g3 = dot(k[...], w3[...]) * scale
    g3_ref[...] = g3
    cv.wait()
    cr.wait()
    rate = jnp.broadcast_to(r_ref[...], (128, r_ref.shape[1])).T[:, :1]
    go = (-(rate * v[...].astype(F32))).astype(BF)
    go_ref[...] = go
    hidden = (g1 * jax.nn.sigmoid(g1) * g3).astype(BF)
    whole[...] = (dot_tn(hidden, go) * scale).astype(BF)
    put_pieces(whole, pieces, PLANS["A"])
    for copy in cq:
        copy.wait()


def grad_one_kernel(k, w2, g1_ref, g3_ref, go_ref, *refs):
    one, three, (dg1, dg3, whole) = refs[:4], refs[4:8], refs[8:]
    scale = w2.shape[-1] ** (-0.5)
    dh = dot_nt(go_ref[...], w2[...]) * scale
    g1 = g1_ref[...]
    sig = jax.nn.sigmoid(g1)
    dg1[...] = (dh * g3_ref[...] * sig * (1.0 + g1 * (1.0 - sig))).astype(BF)
    dg3[...] = (dh * (g1 * sig)).astype(BF)
    whole[...] = (dot_tn(k[...], dg1[...]) * scale).astype(BF)
    put_pieces(whole, one, PLANS["B"])
    whole[...] = (dot_tn(k[...], dg3[...]) * scale).astype(BF)
    put_pieces(whole, three, PLANS["C"])


def normalized(grad):
    grad = grad.astype(F32)
    total = jnp.sum(grad * grad)
    return (grad / (jnp.sqrt(total) + 1e-07)).astype(BF)


def polynomial(gram, square):
    return (coef_b * gram.astype(F32) + coef_c * square).astype(BF)


def step(x):
    half = x.shape[0] // 2
    x0, x1 = x[:half], x[half:]
    cat = jnp.concatenate
    a00 = dot_nt(x0, x0).astype(BF)
    a01 = dot_nt(x0, x1).astype(BF)
    a11 = dot_nt(x1, x1).astype(BF)
    a0 = cat([a00, a01], 1)
    a1 = cat([a01.T, a11], 1)
    b00 = polynomial(a00, dot_nt(a0, a0))
    b01 = polynomial(a01, dot_nt(a0, a1))
    b11 = polynomial(a11, dot_nt(a1, a1))
    b0 = cat([b00, b01], 1)
    b1 = cat([b01.T, b11], 1)
    y0 = (coef_a * x0.astype(F32) + dot(b0, x)).astype(BF)
    y1 = (coef_a * x1.astype(F32) + dot(b1, x)).astype(BF)
    return cat([y0, y1], 0)


def orthogonalize(*grads):
    xs = [normalized(grad) for grad in grads]
    for _ in range(NS_STEPS):
        xs = [step(x) for x in xs]
    return xs


def updated(weight, x):
    step_size = 0.4 * math.sqrt(x.shape[-1])
    return (weight.astype(F32) - step_size * x.astype(F32)).astype(BF)


def first_update_kernel(p0, p1, p2, p3, w, o_ref, whole):
    take_pieces((p0, p1, p2, p3), whole, PLANS["A"])
    (x,) = orthogonalize(whole[...])
    o_ref[...] = updated(w[...], x)


def core():
    return lax.axis_index("ctx") & 1


def pair_update_kernel(p0, p2, p1, p3, w1, w3, o_ref, whole):
    pieces = (p0, p1, p2, p3)

    @pl.when(core() == 0)
    def _():
        take_pieces(pieces, whole, PLANS["B"])

    @pl.when(core() == 1)
    def _():
        take_pieces(pieces, whole, PLANS["C"])

    (x,) = orthogonalize(whole[...])
    o_ref[...] = updated(jnp.where(core() == 0, w1[...], w3[...]), x)


def last_kernel(theirs, partial, o_hbm, sems):
    del partial
    (copy,) = copies([(theirs, o_hbm.at[0, 1 - core()])], sems)
    copy.wait()


def read_kernel(heads, gate_hbm, gain_hbm, w1, w3, w2, *refs):
    gate, gain, sems = refs[2 * heads :]
    made = copies([(gate_hbm, gate), (gain_hbm, gain)], sems)
    scale = w1.shape[-1] ** (-0.5)
    for q, out in zip(refs[:heads], refs[heads : 2 * heads]):
        rows = q[...]
        r1 = dot(rows, w1[...]) * scale
        r3 = dot(rows, w3[...]) * scale
        hq = (r1 * jax.nn.sigmoid(r1) * r3).astype(BF)
        out[...] = (dot(hq, w2[...]) * scale).astype(BF)
    for copy in made:
        copy.wait()


def norm_kernel(heads, gate, gain, mine, two, *refs):
    reads, (out, o_hbm, sems) = refs[:heads], refs[heads:]
    made = copies([(mine, o_hbm.at[0, core()]), (two, o_hbm.at[0, 2])], sems)
    width = reads[0].shape[-1]
    me = lax.axis_index("head")
    for r, read in enumerate(reads):
        at = pl.multiple_of(lax.rem(me + r, heads) * width, width)
        x = read[...].astype(F32)
        mean = jnp.mean(x * x, axis=-1, keepdims=True)
        g = gate[:, pl.ds(at, width)].astype(F32)
        out[:, pl.ds(at, width)] = (
            x * lax.rsqrt(mean + 1e-06) * gain[:, pl.ds(at, width)] * (g * jax.nn.sigmoid(g))
        ).astype(BF)
    for copy in made:
        copy.wait()


def local(ctx, heads, keys, values, rates, queries, fast_weights, gate, gain):
    tok, width = keys.shape
    bits = range(ctx.bit_length() - 1)
    piece = jax.ShapeDtypeStruct((width // 4, width), BF)
    matrix = jax.ShapeDtypeStruct((width, width), BF)
    mat = lambda dtype: pltpu.VMEM((width, width), dtype)
    tokens = lambda dtype: pltpu.VMEM((tok, width), dtype)
    sems = lambda n: pltpu.SemaphoreType.DMA((n,))

    hbm = lambda x: pltpu.with_memory_space_constraint(x, pltpu.HBM)

    def call(kernel, mib, **kw):
        def run(*args):
            return pl.pallas_call(
                kernel, compiler_params=pltpu.CompilerParams(vmem_limit_bytes=mib * MIB), **kw
            )(*args)

        return run

    def swap(x, bit):
        return lax.ppermute(x, "ctx", [(i, i ^ (1 << bit)) for i in range(ctx)])

    def turn(x, r):
        return lax.ppermute(x, "head", [(i, (i + r) % heads) for i in range(heads)])

    outs = call(
        functools.partial(grad_two_kernel, heads), 14,
        out_shape=[piece] * 4
        + [jax.ShapeDtypeStruct((tok, width), d) for d in (F32, F32, BF)]
        + [jax.ShapeDtypeStruct((tok, width), BF)]
        + [matrix] * 3
        + [jax.ShapeDtypeStruct((queries.shape[0], width), BF)] * heads,
        in_specs=[HBM] * 5,
        out_specs=[VM] * (11 + heads),
        scratch_shapes=[tokens(BF), pltpu.VMEM(rates.shape, F32), mat(BF), sems(6 + heads)],
    )(hbm(keys), hbm(values), hbm(rates), hbm(fast_weights), hbm(queries))
    two, (g1, g3, go), (k, w1, w3, w2), columns = outs[:4], outs[4:7], outs[7:11], outs[11:]
    asked = [columns[0]] + [turn(columns[r], r) for r in range(1, heads)]
    outs = call(
        grad_one_kernel, 12,
        out_shape=[piece] * 8,
        in_specs=[VM] * 5,
        out_specs=[VM] * 8,
        scratch_shapes=[tokens(BF), tokens(BF), mat(BF)],
    )(k, w2, g1, g3, go)
    one, three = outs[:4], outs[4:]

    def add(x, y):
        return (x.astype(F32) + y.astype(F32)).astype(BF)

    def summed(n, p):
        plan = PLANS[n]
        far = swap(p[3], 0)
        near = swap(p[1], 0)
        give = add(p[2], far)
        keep = add(p[0], near)
        total = add(keep, swap(give, plan[1]))
        if len(plan) == 3:
            half = total.shape[0] // 2
            total = add(total[:half], swap(total[half:], plan[2]))
        for bit in bits:
            if bit not in plan:
                total = add(total, swap(total, bit))
        if len(plan) == 3:
            total = jnp.concatenate([total, swap(total, plan[2])])
        return total, swap(total, plan[1])

    two, one, three = summed("A", two), summed("B", one), summed("C", three)

    def gathered(own):
        other = [swap(x, 0) for x in own]
        return own[0], other[0], own[1], other[1]

    new_two = call(
        first_update_kernel, 10,
        out_shape=matrix,
        in_specs=[VM] * 5,
        out_specs=VM,
        scratch_shapes=[mat(BF)],
    )(*gathered(two), w2)
    give = [jnp.where(core() == 0, c, b) for b, c in zip(one, three)]
    keep = [jnp.where(core() == 0, b, c) for b, c in zip(one, three)]
    got = [swap(x, 0) for x in give]
    mine = call(
        pair_update_kernel, 10,
        out_shape=matrix,
        in_specs=[VM] * 6,
        out_specs=VM,
        scratch_shapes=[mat(BF)],
    )(*keep, *got, w1, w3)
    theirs = swap(mine, 0)

    gains = gain.reshape(1, -1)
    *reads, gate_here, gain_here = call(
        functools.partial(read_kernel, heads), 12,
        out_shape=[jax.ShapeDtypeStruct(x.shape, BF) for x in asked]
        + [jax.ShapeDtypeStruct(x.shape, x.dtype) for x in (gate, gains)],
        in_specs=[HBM] * 2 + [VM] * (3 + heads),
        out_specs=[VM] * (heads + 2),
        scratch_shapes=[sems(2)],
    )(hbm(gate), hbm(gains), w1, w3, w2, *asked)
    back = [reads[0]] + [turn(reads[r], heads - r) for r in range(1, heads)]
    layer_out, new_weights = call(
        functools.partial(norm_kernel, heads), 8,
        out_shape=[
            jax.ShapeDtypeStruct(queries.shape, BF),
            jax.ShapeDtypeStruct(fast_weights.shape, BF),
        ],
        in_specs=[VM] * (4 + heads),
        out_specs=[VM, HBM],
        scratch_shapes=[sems(2)],
    )(gate_here, gain_here, mine, new_two, *back)
    new_weights = call(
        last_kernel, 4,
        out_shape=jax.ShapeDtypeStruct(fast_weights.shape, BF),
        in_specs=[VM, HBM],
        out_specs=HBM,
        scratch_shapes=[sems(1)],
        input_output_aliases={1: 0},
    )(theirs, new_weights)
    return layer_out, new_weights


def solution(mesh):
    in_specs = (
        P("ctx", "head"),
        P("ctx", "head"),
        P("head", "ctx"),
        P(("ctx", "head"), None),
        P("head", None, None, None),
        P(("ctx", "head"), None),
        P(),
    )
    out_specs = (P(("ctx", "head"), None), P("head", None, None, None))

    def body(*args):
        return local(mesh.shape["ctx"], mesh.shape["head"], *args)

    return jax.shard_map(
        body, mesh=mesh, in_specs=in_specs, out_specs=out_specs, check_vma=False
    )
```

```python
import functools
import math

import jax
import jax.numpy as jnp
from jax import lax
from jax.experimental import pallas as pl
from jax.experimental.pallas import tpu as pltpu
from jax.sharding import PartitionSpec as P


NS_STEPS = 5
coef_a = 3.4445
coef_b = -4.775
coef_c = 2.0315
PLANS = {'A': (0, 1, 2), 'B': (0, 2, 1), 'C': (0, 1)}
BF = jnp.bfloat16
F32 = jnp.float32
MIB = 1 << 20
ANY = pl.BlockSpec(memory_space=pl.ANY)
HBM = pl.BlockSpec(memory_space=pltpu.HBM)
VM = pl.BlockSpec(memory_space=pltpu.VMEM)


def dot(left, right):
    return jnp.dot(left, right, preferred_element_type=F32)


def dot_nt(left, right):
    return lax.dot_general(left, right, (((1,), (1,)), ((), ())), preferred_element_type=F32)


def dot_tn(left, right):
    return lax.dot_general(left, right, (((0,), (0,)), ((), ())), preferred_element_type=F32)


def copies(pairs, sems):
    made = [pltpu.make_async_copy(src, dst, sems.at[i]) for i, (src, dst) in enumerate(pairs)]
    for copy in made:
        copy.start()
    return made


def blocks(whole, bits):
    index = lax.axis_index("ctx")
    own = sum(((index >> b) & 1) << i for i, b in enumerate(bits))
    parts = 1 << (len(bits) - 2)
    rows = whole.shape[0] // (4 * parts)
    for r in range(4):
        for e in range(parts):
            at = pl.multiple_of((own ^ (r | (e << 2))) * rows, rows)
            yield r, pl.ds(e * rows, rows), pl.ds(at, rows)


def put_pieces(whole, halves, bits):
    quarter = whole.shape[0] // 4
    for r, part, rows in blocks(whole, bits):
        half = halves[r & 1].at[pl.ds((r >> 1) * quarter, quarter), :]
        half[part, :] = whole[rows, :]


def take_pieces(pieces, whole, bits):
    for r, part, rows in blocks(whole, bits):
        whole[rows, :] = pieces[r][part, :]


def token_spans(tokens):
    return [slice(0, tokens // 2), slice(tokens // 2, tokens)]


def grad_two_kernel(heads, k_hbm, v_hbm, r_hbm, w_hbm, q_hbm, *refs):
    halves, (g1_ref, g3_ref, go_ref), (k, w2) = refs[:2], refs[2:5], refs[5:7]
    asked = refs[7 : 7 + heads]
    v, r_ref, w1, w3, whole, sems = refs[7 + heads :]
    width = w1.shape[-1]
    me = lax.axis_index("head")
    columns = []
    for r, out in enumerate(asked):
        at = pl.multiple_of(lax.rem(me + r, heads) * width, width)
        columns.append((q_hbm.at[:, pl.ds(at, width)], out))
    ck, c1, c3, cv, cr = copies(
        [(k_hbm, k), (w_hbm.at[0, 0], w1), (w_hbm.at[0, 1], w3), (v_hbm, v), (r_hbm, r_ref)], sems
    )
    scale = w1.shape[-1] ** (-0.5)
    ck.wait()
    c1.wait()
    later = copies([(w_hbm.at[0, 2], w2)] + columns, sems.at[pl.ds(5, 1 + heads)])
    spans = token_spans(k.shape[0])
    g1 = []
    for rows in spans:
        g1.append(dot(k[rows, :], w1[...]) * scale)
        g1_ref[rows, :] = g1[-1]
    c3.wait()
    cv.wait()
    cr.wait()
    rate = jnp.broadcast_to(r_ref[...], (128, r_ref.shape[1])).T[:, :1]
    total = None
    for rows, one in zip(spans, g1):
        three = dot(k[rows, :], w3[...]) * scale
        g3_ref[rows, :] = three
        go = (-(rate[rows, :] * v[rows, :].astype(F32))).astype(BF)
        go_ref[rows, :] = go
        hidden = (one * jax.nn.sigmoid(one) * three).astype(BF)
        part = dot_tn(hidden, go)
        total = part if total is None else total + part
    whole[...] = (total * scale).astype(BF)
    put_pieces(whole, halves, PLANS["A"])
    for copy in later:
        copy.wait()


def grad_one_kernel(k, w2, g1_ref, g3_ref, go_ref, *refs):
    one, three, (dg1, dg3, whole) = refs[:2], refs[2:4], refs[4:]
    scale = w2.shape[-1] ** (-0.5)
    for rows in token_spans(k.shape[0]):
        dh = dot_nt(go_ref[rows, :], w2[...]) * scale
        g1 = g1_ref[rows, :]
        sig = jax.nn.sigmoid(g1)
        dg1[rows, :] = (dh * g3_ref[rows, :] * sig * (1.0 + g1 * (1.0 - sig))).astype(BF)
        dg3[rows, :] = (dh * (g1 * sig)).astype(BF)
    whole[...] = (dot_tn(k[...], dg1[...]) * scale).astype(BF)
    put_pieces(whole, one, PLANS["B"])
    whole[...] = (dot_tn(k[...], dg3[...]) * scale).astype(BF)
    put_pieces(whole, three, PLANS["C"])


def normalized(grad):
    grad = grad.astype(F32)
    total = jnp.sum(grad * grad)
    return (grad / (jnp.sqrt(total) + 1e-07)).astype(BF)


def polynomial(gram, square):
    return (coef_b * gram.astype(F32) + coef_c * square).astype(BF)


def step(x):
    half = x.shape[0] // 2
    x0, x1 = x[:half], x[half:]
    cat = jnp.concatenate
    a00 = dot_nt(x0, x0).astype(BF)
    a01 = dot_nt(x0, x1).astype(BF)
    a11 = dot_nt(x1, x1).astype(BF)
    a0 = cat([a00, a01], 1)
    a1 = cat([a01.T, a11], 1)
    b00 = polynomial(a00, dot_nt(a0, a0))
    b01 = polynomial(a01, dot_nt(a0, a1))
    b11 = polynomial(a11, dot_nt(a1, a1))
    b0 = cat([b00, b01], 1)
    b1 = cat([b01.T, b11], 1)
    y0 = (coef_a * x0.astype(F32) + dot(b0, x)).astype(BF)
    y1 = (coef_a * x1.astype(F32) + dot(b1, x)).astype(BF)
    return cat([y0, y1], 0)


def orthogonalize(*grads):
    xs = [normalized(grad) for grad in grads]
    for _ in range(NS_STEPS):
        xs = [step(x) for x in xs]
    return xs


def updated(weight, x):
    step_size = 0.4 * math.sqrt(x.shape[-1])
    return (weight.astype(F32) - step_size * x.astype(F32)).astype(BF)


def first_update_kernel(p0, p1, p2, p3, w_hbm, gate_hbm, gain_hbm, o_ref, gate, gain, w, whole, sems):
    cw, *made = copies([(w_hbm.at[0, 2], w), (gate_hbm, gate), (gain_hbm, gain)], sems)
    take_pieces((p0, p1, p2, p3), whole, PLANS["A"])
    (x,) = orthogonalize(whole[...])
    cw.wait()
    o_ref[...] = updated(w[...], x)
    for copy in made:
        copy.wait()


def core():
    return lax.axis_index("ctx") & 1


def pair_update_kernel(p0, p2, p1, p3, w_hbm, o_ref, w, whole, sems):
    (cw,) = copies([(w_hbm.at[0, core()], w)], sems)
    pieces = (p0, p1, p2, p3)

    @pl.when(core() == 0)
    def _():
        take_pieces(pieces, whole, PLANS["B"])

    @pl.when(core() == 1)
    def _():
        take_pieces(pieces, whole, PLANS["C"])

    (x,) = orthogonalize(whole[...])
    cw.wait()
    o_ref[...] = updated(w[...], x)


def last_kernel(theirs, partial, o_hbm, sems):
    del partial
    (copy,) = copies([(theirs, o_hbm.at[0, 1 - core()])], sems)
    copy.wait()


def read_kernel(heads, w_hbm, *refs):
    queries, reads, (w1, w3, w2, sems) = refs[:heads], refs[heads : 2 * heads], refs[2 * heads :]
    c1, c3, c2 = copies([(w_hbm.at[0, i], w) for i, w in enumerate((w1, w3, w2))], sems)
    scale = w1.shape[-1] ** (-0.5)
    c1.wait()
    r1 = [dot(q[...], w1[...]) * scale for q in queries]
    c3.wait()
    r3 = [dot(q[...], w3[...]) * scale for q in queries]
    hq = [(a * jax.nn.sigmoid(a) * b).astype(BF) for a, b in zip(r1, r3)]
    c2.wait()
    for h, out in zip(hq, reads):
        out[...] = (dot(h, w2[...]) * scale).astype(BF)


def norm_kernel(heads, gate, gain, mine, two, *refs):
    reads, (out, o_hbm, sems) = refs[:heads], refs[heads:]
    made = copies([(mine, o_hbm.at[0, core()]), (two, o_hbm.at[0, 2])], sems)
    width = reads[0].shape[-1]
    me = lax.axis_index("head")
    for r, read in enumerate(reads):
        at = pl.multiple_of(lax.rem(me + r, heads) * width, width)
        x = read[...].astype(F32)
        mean = jnp.mean(x * x, axis=-1, keepdims=True)
        g = gate[:, pl.ds(at, width)].astype(F32)
        out[:, pl.ds(at, width)] = (
            x * lax.rsqrt(mean + 1e-06) * gain[:, pl.ds(at, width)] * (g * jax.nn.sigmoid(g))
        ).astype(BF)
    for copy in made:
        copy.wait()


def local(ctx, heads, keys, values, rates, queries, fast_weights, gate, gain):
    tok, width = keys.shape
    bits = range(ctx.bit_length() - 1)
    halves = jax.ShapeDtypeStruct((width // 2, width), BF)
    matrix = jax.ShapeDtypeStruct((width, width), BF)
    mat = lambda dtype: pltpu.VMEM((width, width), dtype)
    tokens = lambda dtype: pltpu.VMEM((tok, width), dtype)
    sems = lambda n: pltpu.SemaphoreType.DMA((n,))

    hbm = lambda x: pltpu.with_memory_space_constraint(x, pltpu.HBM)

    def call(kernel, mib, **kw):
        def run(*args):
            return pl.pallas_call(
                kernel, compiler_params=pltpu.CompilerParams(vmem_limit_bytes=mib * MIB), **kw
            )(*args)

        return run

    def swap(x, bit):
        return lax.ppermute(x, "ctx", [(i, i ^ (1 << bit)) for i in range(ctx)])

    def turn(x, r):
        return lax.ppermute(x, "head", [(i, (i + r) % heads) for i in range(heads)])

    outs = call(
        functools.partial(grad_two_kernel, heads), 14,
        out_shape=[halves] * 2
        + [jax.ShapeDtypeStruct((tok, width), d) for d in (F32, F32, BF)]
        + [jax.ShapeDtypeStruct((tok, width), BF)]
        + [matrix]
        + [jax.ShapeDtypeStruct((queries.shape[0], width), BF)] * heads,
        in_specs=[HBM] * 5,
        out_specs=[VM] * (7 + heads),
        scratch_shapes=[tokens(BF), pltpu.VMEM(rates.shape, F32), mat(BF), mat(BF), mat(BF), sems(6 + heads)],
    )(hbm(keys), hbm(values), hbm(rates), hbm(fast_weights), hbm(queries))
    two, (g1, g3, go), (k, w2), columns = outs[:2], outs[2:5], outs[5:7], outs[7:]
    asked = [columns[0]] + [turn(columns[r], r) for r in range(1, heads)]
    outs = call(
        grad_one_kernel, 12,
        out_shape=[halves] * 4,
        in_specs=[VM] * 5,
        out_specs=[VM] * 4,
        scratch_shapes=[tokens(BF), tokens(BF), mat(BF)],
    )(k, w2, g1, g3, go)
    one, three = outs[:2], outs[2:]

    def add(x, y):
        return (x.astype(F32) + y.astype(F32)).astype(BF)

    def summed(n, p):
        plan = PLANS[n]
        keep, send = p
        got = swap(send, 0)
        quarter = width // 4

        give = add(keep[quarter:], got[quarter:])
        total, got = add(keep[:quarter], got[:quarter]), swap(give, plan[1])
        if len(plan) == 3:
            half = quarter // 2
            give = add(total[half:], got[half:])
            total, got = add(total[:half], got[:half]), swap(give, plan[2])
        for bit in bits:
            if bit not in plan:
                total = add(total, got)
                got = swap(total, bit)
        if len(plan) == 3:
            total = add(total, got)
            got = swap(total, plan[2])
            total = jnp.concatenate([total, got])
        else:
            total = add(total, got)
        return total, swap(total, plan[1])

    two, one, three = summed("A", two), summed("B", one), summed("C", three)

    def gathered(own):
        other = [swap(x, 0) for x in own]
        return own[0], other[0], own[1], other[1]

    gains = gain.reshape(1, -1)
    new_two, gate_here, gain_here = call(
        first_update_kernel, 10,
        out_shape=[matrix] + [jax.ShapeDtypeStruct(x.shape, x.dtype) for x in (gate, gains)],
        in_specs=[VM] * 4 + [HBM] * 3,
        out_specs=[VM] * 3,
        scratch_shapes=[mat(BF), mat(BF), sems(3)],
    )(*gathered(two), hbm(fast_weights), hbm(gate), hbm(gains))
    keep, got = [], []
    for b, c in zip(one, three):
        keep.append(jnp.where(core() == 0, b, c))
        give = lax.select_n(jnp.broadcast_to(core() == 0, b.shape), b, c)
        got.append(swap(give, 0))
    mine = call(
        pair_update_kernel, 10,
        out_shape=matrix,
        in_specs=[VM] * 4 + [HBM],
        out_specs=VM,
        scratch_shapes=[mat(BF), mat(BF), sems(1)],
    )(*keep, *got, hbm(fast_weights))
    theirs = swap(mine, 0)

    reads = call(
        functools.partial(read_kernel, heads), 12,
        out_shape=[jax.ShapeDtypeStruct(x.shape, BF) for x in asked],
        in_specs=[HBM] + [VM] * heads,
        out_specs=[VM] * heads,
        scratch_shapes=[mat(BF)] * 3 + [sems(3)],
    )(hbm(fast_weights), *asked)
    back = [reads[0]] + [turn(reads[r], heads - r) for r in range(1, heads)]
    layer_out, new_weights = call(
        functools.partial(norm_kernel, heads), 8,
        out_shape=[
            jax.ShapeDtypeStruct(queries.shape, BF),
            jax.ShapeDtypeStruct(fast_weights.shape, BF),
        ],
        in_specs=[VM] * (4 + heads),
        out_specs=[VM, HBM],
        scratch_shapes=[sems(2)],
    )(gate_here, gain_here, mine, new_two, *back)
    new_weights = call(
        last_kernel, 4,
        out_shape=jax.ShapeDtypeStruct(fast_weights.shape, BF),
        in_specs=[VM, HBM],
        out_specs=HBM,
        scratch_shapes=[sems(1)],
        input_output_aliases={1: 0},
    )(theirs, new_weights)
    return layer_out, new_weights


def solution(mesh):
    in_specs = (
        P("ctx", "head"),
        P("ctx", "head"),
        P("head", "ctx"),
        P(("ctx", "head"), None),
        P("head", None, None, None),
        P(("ctx", "head"), None),
        P(),
    )
    out_specs = (P(("ctx", "head"), None), P("head", None, None, None))

    def body(*args):
        return local(mesh.shape["ctx"], mesh.shape["head"], *args)

    return jax.shard_map(
        body, mesh=mesh, in_specs=in_specs, out_specs=out_specs, check_vma=False
    )
```

```python
import functools
import math

import jax
import jax.numpy as jnp
from jax import lax
from jax.experimental import pallas as pl
from jax.experimental.pallas import tpu as pltpu
from jax.sharding import PartitionSpec as P


NS_STEPS = 5
FIRST_STEPS = 4
coef_a = 3.4445
coef_b = -4.775
coef_c = 2.0315
PLANS = {'A': (0, 1, 2), 'B': (0, 2, 1), 'C': (0, 1)}
BF = jnp.bfloat16
F32 = jnp.float32
MIB = 1 << 20
ANY = pl.BlockSpec(memory_space=pl.ANY)
HBM = pl.BlockSpec(memory_space=pltpu.HBM)
VM = pl.BlockSpec(memory_space=pltpu.VMEM)


def dot(left, right):
    return jnp.dot(left, right, preferred_element_type=F32)


def dot_nt(left, right):
    return lax.dot_general(left, right, (((1,), (1,)), ((), ())), preferred_element_type=F32)


def dot_tn(left, right):
    return lax.dot_general(left, right, (((0,), (0,)), ((), ())), preferred_element_type=F32)


def copies(pairs, sems):
    made = [pltpu.make_async_copy(src, dst, sems.at[i]) for i, (src, dst) in enumerate(pairs)]
    for copy in made:
        copy.start()
    return made


def blocks(whole, bits):
    index = lax.axis_index("ctx")
    own = sum(((index >> b) & 1) << i for i, b in enumerate(bits))
    parts = 1 << (len(bits) - 2)
    rows = whole.shape[0] // (4 * parts)
    for r in range(4):
        for e in range(parts):
            at = pl.multiple_of((own ^ (r | (e << 2))) * rows, rows)
            yield r, pl.ds(e * rows, rows), pl.ds(at, rows)


def put_pieces(whole, halves, bits):
    quarter = whole.shape[0] // 4
    for r, part, rows in blocks(whole, bits):
        half = halves[r & 1].at[pl.ds((r >> 1) * quarter, quarter), :]
        half[part, :] = whole[rows, :]


def take_pieces(pieces, whole, bits):
    for r, part, rows in blocks(whole, bits):
        whole[rows, :] = pieces[r][part, :]


def token_spans(tokens):
    return [slice(0, tokens // 2), slice(tokens // 2, tokens)]


def grad_two_kernel(heads, k_hbm, v_hbm, r_hbm, w_hbm, q_hbm, *refs):
    halves, (g1_ref, g3_ref, go_ref), (k, w2) = refs[:2], refs[2:5], refs[5:7]
    asked = refs[7 : 7 + heads]
    v, r_ref, w1, w3, whole, sems = refs[7 + heads :]
    width = w1.shape[-1]
    me = lax.axis_index("head")
    columns = []
    for r, out in enumerate(asked):
        at = pl.multiple_of(lax.rem(me + r, heads) * width, width)
        columns.append((q_hbm.at[:, pl.ds(at, width)], out))
    ck, c1, c3, cv, cr = copies(
        [(k_hbm, k), (w_hbm.at[0, 0], w1), (w_hbm.at[0, 1], w3), (v_hbm, v), (r_hbm, r_ref)], sems
    )
    scale = w1.shape[-1] ** (-0.5)
    ck.wait()
    c1.wait()
    later = copies([(w_hbm.at[0, 2], w2)] + columns, sems.at[pl.ds(5, 1 + heads)])
    spans = token_spans(k.shape[0])
    g1 = []
    for rows in spans:
        g1.append(dot(k[rows, :], w1[...]) * scale)
        g1_ref[rows, :] = g1[-1]
    c3.wait()
    cv.wait()
    cr.wait()
    rate = jnp.broadcast_to(r_ref[...], (128, r_ref.shape[1])).T[:, :1]
    total = None
    for rows, one in zip(spans, g1):
        three = dot(k[rows, :], w3[...]) * scale
        g3_ref[rows, :] = three
        go = (-(rate[rows, :] * v[rows, :].astype(F32))).astype(BF)
        go_ref[rows, :] = go
        hidden = (one * jax.nn.sigmoid(one) * three).astype(BF)
        part = dot_tn(hidden, go)
        total = part if total is None else total + part
    whole[...] = (total * scale).astype(BF)
    put_pieces(whole, halves, PLANS["A"])
    for copy in later:
        copy.wait()


def grad_one_kernel(k, w2, g1_ref, g3_ref, go_ref, *refs):
    one, three, (dg1, dg3, whole) = refs[:2], refs[2:4], refs[4:]
    scale = w2.shape[-1] ** (-0.5)
    for rows in token_spans(k.shape[0]):
        dh = dot_nt(go_ref[rows, :], w2[...]) * scale
        g1 = g1_ref[rows, :]
        sig = jax.nn.sigmoid(g1)
        dg1[rows, :] = (dh * g3_ref[rows, :] * sig * (1.0 + g1 * (1.0 - sig))).astype(BF)
        dg3[rows, :] = (dh * (g1 * sig)).astype(BF)
    whole[...] = (dot_tn(k[...], dg1[...]) * scale).astype(BF)
    put_pieces(whole, one, PLANS["B"])
    whole[...] = (dot_tn(k[...], dg3[...]) * scale).astype(BF)
    put_pieces(whole, three, PLANS["C"])


def normalized(grad):
    grad = grad.astype(F32)
    total = jnp.sum(grad * grad)
    return (grad / (jnp.sqrt(total) + 1e-07)).astype(BF)


def polynomial(gram, square):
    return (coef_b * gram.astype(F32) + coef_c * square).astype(BF)


def step(x):
    half = x.shape[0] // 2
    cat = jnp.concatenate
    gram = dot_nt(x, x).astype(BF)
    upper, lower = gram[:half], gram[half:]
    b01 = polynomial(upper[:, half:], dot(upper, gram[:, half:]))
    b10 = b01.T
    b00 = polynomial(upper[:, :half], dot(upper, gram[:, :half]))
    b11 = polynomial(lower[:, half:], dot(lower, gram[:, half:]))
    y0 = coef_a * x[:half].astype(F32) + dot(cat([b00, b01], 1), x)
    y1 = coef_a * x[half:].astype(F32) + dot(cat([b10, b11], 1), x)
    return cat([y0.astype(BF), y1.astype(BF)], 0)


def steps(x, count):
    for _ in range(count):
        x = step(x)
    return x


def updated(weight, x):
    step_size = 0.4 * math.sqrt(x.shape[-1])
    return (weight.astype(F32) - step_size * x.astype(F32)).astype(BF)


def first_steps_kernel(p0, p1, p2, p3, gate_hbm, gain_hbm, o_ref, gate, gain, whole, sems):
    made = copies([(gate_hbm, gate), (gain_hbm, gain)], sems)
    take_pieces((p0, p1, p2, p3), whole, PLANS["A"])
    o_ref[...] = steps(normalized(whole[...]), FIRST_STEPS)
    for copy in made:
        copy.wait()


def first_update_kernel(x_ref, w_hbm, o_ref, w, sems):
    (cw,) = copies([(w_hbm.at[0, 2], w)], sems)
    x = steps(x_ref[...], NS_STEPS - FIRST_STEPS)
    cw.wait()
    o_ref[...] = updated(w[...], x)


def core():
    return lax.axis_index("ctx") & 1


def pair_update_kernel(p0, p2, p1, p3, w_hbm, o_ref, w, whole, sems):
    (cw,) = copies([(w_hbm.at[0, core()], w)], sems)
    pieces = (p0, p1, p2, p3)

    @pl.when(core() == 0)
    def _():
        take_pieces(pieces, whole, PLANS["B"])

    @pl.when(core() == 1)
    def _():
        take_pieces(pieces, whole, PLANS["C"])

    x = steps(normalized(whole[...]), NS_STEPS)
    cw.wait()
    o_ref[...] = updated(w[...], x)


def last_kernel(theirs, partial, o_hbm, sems):
    del partial
    (copy,) = copies([(theirs, o_hbm.at[0, 1 - core()])], sems)
    copy.wait()


def read_kernel(heads, w_hbm, *refs):
    queries, reads, (w1, w3, w2, sems) = refs[:heads], refs[heads : 2 * heads], refs[2 * heads :]
    c1, c3, c2 = copies([(w_hbm.at[0, i], w) for i, w in enumerate((w1, w3, w2))], sems)
    scale = w1.shape[-1] ** (-0.5)
    c1.wait()
    r1 = [dot(q[...], w1[...]) * scale for q in queries]
    c3.wait()
    r3 = [dot(q[...], w3[...]) * scale for q in queries]
    hq = [(a * jax.nn.sigmoid(a) * b).astype(BF) for a, b in zip(r1, r3)]
    c2.wait()
    for h, out in zip(hq, reads):
        out[...] = (dot(h, w2[...]) * scale).astype(BF)


def norm_kernel(heads, gate, gain, mine, two, *refs):
    reads, (out, o_hbm, sems) = refs[:heads], refs[heads:]
    made = copies([(mine, o_hbm.at[0, core()]), (two, o_hbm.at[0, 2])], sems)
    width = reads[0].shape[-1]
    me = lax.axis_index("head")
    for r, read in enumerate(reads):
        at = pl.multiple_of(lax.rem(me + r, heads) * width, width)
        x = read[...].astype(F32)
        mean = jnp.mean(x * x, axis=-1, keepdims=True)
        g = gate[:, pl.ds(at, width)].astype(F32)
        out[:, pl.ds(at, width)] = (
            x * lax.rsqrt(mean + 1e-06) * gain[:, pl.ds(at, width)] * (g * jax.nn.sigmoid(g))
        ).astype(BF)
    for copy in made:
        copy.wait()


def local(ctx, heads, keys, values, rates, queries, fast_weights, gate, gain):
    tok, width = keys.shape
    bits = range(ctx.bit_length() - 1)
    halves = jax.ShapeDtypeStruct((width // 2, width), BF)
    matrix = jax.ShapeDtypeStruct((width, width), BF)
    mat = lambda dtype: pltpu.VMEM((width, width), dtype)
    tokens = lambda dtype: pltpu.VMEM((tok, width), dtype)
    sems = lambda n: pltpu.SemaphoreType.DMA((n,))

    hbm = lambda x: pltpu.with_memory_space_constraint(x, pltpu.HBM)

    def call(kernel, mib, **kw):
        def run(*args):
            return pl.pallas_call(
                kernel, compiler_params=pltpu.CompilerParams(vmem_limit_bytes=mib * MIB), **kw
            )(*args)

        return run

    def swap(x, bit):
        return lax.ppermute(x, "ctx", [(i, i ^ (1 << bit)) for i in range(ctx)])

    def turn(x, r):
        return lax.ppermute(x, "head", [(i, (i + r) % heads) for i in range(heads)])

    outs = call(
        functools.partial(grad_two_kernel, heads), 14,
        out_shape=[halves] * 2
        + [jax.ShapeDtypeStruct((tok, width), d) for d in (F32, F32, BF)]
        + [jax.ShapeDtypeStruct((tok, width), BF)]
        + [matrix]
        + [jax.ShapeDtypeStruct((queries.shape[0], width), BF)] * heads,
        in_specs=[HBM] * 5,
        out_specs=[VM] * (7 + heads),
        scratch_shapes=[tokens(BF), pltpu.VMEM(rates.shape, F32), mat(BF), mat(BF), mat(BF), sems(6 + heads)],
    )(hbm(keys), hbm(values), hbm(rates), hbm(fast_weights), hbm(queries))
    two, (g1, g3, go), (k, w2), columns = outs[:2], outs[2:5], outs[5:7], outs[7:]
    asked = [columns[0]] + [turn(columns[r], r) for r in range(1, heads)]
    outs = call(
        grad_one_kernel, 12,
        out_shape=[halves] * 4,
        in_specs=[VM] * 5,
        out_specs=[VM] * 4,
        scratch_shapes=[tokens(BF), tokens(BF), mat(BF)],
    )(k, w2, g1, g3, go)
    one, three = outs[:2], outs[2:]

    def add(x, y):
        return (x.astype(F32) + y.astype(F32)).astype(BF)

    def summed(n, p):
        plan = PLANS[n]
        keep, send = p
        got = swap(send, 0)
        quarter = width // 4

        give = add(keep[quarter:], got[quarter:])
        total, got = add(keep[:quarter], got[:quarter]), swap(give, plan[1])
        if len(plan) == 3:
            half = quarter // 2
            give = add(total[half:], got[half:])
            total, got = add(total[:half], got[:half]), swap(give, plan[2])
        for bit in bits:
            if bit not in plan:
                total = add(total, got)
                got = swap(total, bit)
        if len(plan) == 3:
            total = add(total, got)
            got = swap(total, plan[2])
            total = jnp.concatenate([total, got])
        else:
            total = add(total, got)
        return total, swap(total, plan[1])

    two, one, three = summed("A", two), summed("B", one), summed("C", three)

    def gathered(own):
        other = [swap(x, 0) for x in own]
        return own[0], other[0], own[1], other[1]

    gains = gain.reshape(1, -1)
    x_two, gate_here, gain_here = call(
        first_steps_kernel, 10,
        out_shape=[matrix] + [jax.ShapeDtypeStruct(x.shape, x.dtype) for x in (gate, gains)],
        in_specs=[VM] * 4 + [HBM] * 2,
        out_specs=[VM] * 3,
        scratch_shapes=[mat(BF), sems(2)],
    )(*gathered(two), hbm(gate), hbm(gains))
    new_two = call(
        first_update_kernel, 10,
        out_shape=matrix,
        in_specs=[VM, HBM],
        out_specs=VM,
        scratch_shapes=[mat(BF), sems(1)],
    )(x_two, hbm(fast_weights))
    keep, got = [], []
    for b, c in zip(one, three):
        keep.append(jnp.where(core() == 0, b, c))
        give = lax.select_n(jnp.broadcast_to(core() == 0, b.shape), b, c)
        got.append(swap(give, 0))
    mine = call(
        pair_update_kernel, 10,
        out_shape=matrix,
        in_specs=[VM] * 4 + [HBM],
        out_specs=VM,
        scratch_shapes=[mat(BF), mat(BF), sems(1)],
    )(*keep, *got, hbm(fast_weights))
    theirs = swap(mine, 0)

    reads = call(
        functools.partial(read_kernel, heads), 12,
        out_shape=[jax.ShapeDtypeStruct(x.shape, BF) for x in asked],
        in_specs=[HBM] + [VM] * heads,
        out_specs=[VM] * heads,
        scratch_shapes=[mat(BF)] * 3 + [sems(3)],
    )(hbm(fast_weights), *asked)
    back = [reads[0]] + [turn(reads[r], heads - r) for r in range(1, heads)]
    layer_out, new_weights = call(
        functools.partial(norm_kernel, heads), 8,
        out_shape=[
            jax.ShapeDtypeStruct(queries.shape, BF),
            jax.ShapeDtypeStruct(fast_weights.shape, BF),
        ],
        in_specs=[VM] * (4 + heads),
        out_specs=[VM, HBM],
        scratch_shapes=[sems(2)],
    )(gate_here, gain_here, mine, new_two, *back)
    new_weights = call(
        last_kernel, 4,
        out_shape=jax.ShapeDtypeStruct(fast_weights.shape, BF),
        in_specs=[VM, HBM],
        out_specs=HBM,
        scratch_shapes=[sems(1)],
        input_output_aliases={1: 0},
    )(theirs, new_weights)
    return layer_out, new_weights


def solution(mesh):
    in_specs = (
        P("ctx", "head"),
        P("ctx", "head"),
        P("head", "ctx"),
        P(("ctx", "head"), None),
        P("head", None, None, None),
        P(("ctx", "head"), None),
        P(),
    )
    out_specs = (P(("ctx", "head"), None), P("head", None, None, None))

    def body(*args):
        return local(mesh.shape["ctx"], mesh.shape["head"], *args)

    return jax.shard_map(
        body, mesh=mesh, in_specs=in_specs, out_specs=out_specs, check_vma=False
    )
```

```python
import functools
import math

import jax
import jax.numpy as jnp
from jax import lax
from jax.experimental import pallas as pl
from jax.experimental.pallas import tpu as pltpu
from jax.sharding import PartitionSpec as P


NS_STEPS = 5
FIRST_STEPS = 4
coef_a = 3.4445
coef_b = -4.775
coef_c = 2.0315
PLANS = {'A': (0, 1, 2), 'B': (0, 2, 1), 'C': (0, 1)}
BF = jnp.bfloat16
F32 = jnp.float32
MIB = 1 << 20
ANY = pl.BlockSpec(memory_space=pl.ANY)
HBM = pl.BlockSpec(memory_space=pltpu.HBM)
VM = pl.BlockSpec(memory_space=pltpu.VMEM)


def dot(left, right):
    return jnp.dot(left, right, preferred_element_type=F32)


def dot_nt(left, right):
    return lax.dot_general(left, right, (((1,), (1,)), ((), ())), preferred_element_type=F32)


def dot_tn(left, right):
    return lax.dot_general(left, right, (((0,), (0,)), ((), ())), preferred_element_type=F32)


def copies(pairs, sems):
    made = [pltpu.make_async_copy(src, dst, sems.at[i]) for i, (src, dst) in enumerate(pairs)]
    for copy in made:
        copy.start()
    return made


def blocks(whole, bits):
    index = lax.axis_index("ctx")
    own = sum(((index >> b) & 1) << i for i, b in enumerate(bits))
    parts = 1 << (len(bits) - 2)
    rows = whole.shape[0] // (4 * parts)
    for r in range(4):
        for e in range(parts):
            at = pl.multiple_of((own ^ (r | (e << 2))) * rows, rows)
            yield r, pl.ds(e * rows, rows), pl.ds(at, rows)


def put_pieces(whole, halves, bits):
    quarter = whole.shape[0] // 4
    for r, part, rows in blocks(whole, bits):
        half = halves[r & 1].at[pl.ds((r >> 1) * quarter, quarter), :]
        half[part, :] = whole[rows, :]


def take_pieces(pieces, whole, bits):
    for r, part, rows in blocks(whole, bits):
        whole[rows, :] = pieces[r][part, :]


def token_spans(tokens):
    return [slice(0, tokens // 2), slice(tokens // 2, tokens)]


def grad_two_kernel(heads, k_hbm, v_hbm, r_hbm, w_hbm, q_hbm, *refs):
    halves, (g1_ref, g3_ref, go_ref), (k, w2) = refs[:2], refs[2:5], refs[5:7]
    asked = refs[7 : 7 + heads]
    v, r_ref, w1, w3, whole, sems = refs[7 + heads :]
    width = w1.shape[-1]
    me = lax.axis_index("head")
    columns = []
    for r, out in enumerate(asked):
        at = pl.multiple_of(lax.rem(me + r, heads) * width, width)
        columns.append((q_hbm.at[:, pl.ds(at, width)], out))
    ck, c1, c3, cv, cr = copies(
        [(k_hbm, k), (w_hbm.at[0, 0], w1), (w_hbm.at[0, 1], w3), (v_hbm, v), (r_hbm, r_ref)], sems
    )
    scale = w1.shape[-1] ** (-0.5)
    ck.wait()
    c1.wait()
    later = copies([(w_hbm.at[0, 2], w2)] + columns, sems.at[pl.ds(5, 1 + heads)])
    spans = token_spans(k.shape[0])
    g1 = []
    for rows in spans:
        g1.append(dot(k[rows, :], w1[...]) * scale)
        g1_ref[rows, :] = g1[-1]
    c3.wait()
    cv.wait()
    cr.wait()
    rate = jnp.broadcast_to(r_ref[...], (128, r_ref.shape[1])).T[:, :1]
    total = None
    for rows, one in zip(spans, g1):
        three = dot(k[rows, :], w3[...]) * scale
        g3_ref[rows, :] = three
        go = (-(rate[rows, :] * v[rows, :].astype(F32))).astype(BF)
        go_ref[rows, :] = go
        hidden = (one * jax.nn.sigmoid(one) * three).astype(BF)
        part = dot_tn(hidden, go)
        total = part if total is None else total + part
    whole[...] = (total * scale).astype(BF)
    put_pieces(whole, halves, PLANS["A"])
    for copy in later:
        copy.wait()


def grad_one_kernel(k, w2, g1_ref, g3_ref, go_ref, *refs):
    one, three, (dg1, dg3, whole) = refs[:2], refs[2:4], refs[4:]
    scale = w2.shape[-1] ** (-0.5)
    for rows in token_spans(k.shape[0]):
        dh = dot_nt(go_ref[rows, :], w2[...]) * scale
        g1 = g1_ref[rows, :]
        sig = jax.nn.sigmoid(g1)
        dg1[rows, :] = (dh * g3_ref[rows, :] * sig * (1.0 + g1 * (1.0 - sig))).astype(BF)
        dg3[rows, :] = (dh * (g1 * sig)).astype(BF)
    whole[...] = (dot_tn(k[...], dg1[...]) * scale).astype(BF)
    put_pieces(whole, one, PLANS["B"])
    whole[...] = (dot_tn(k[...], dg3[...]) * scale).astype(BF)
    put_pieces(whole, three, PLANS["C"])


def normalized(grad):
    grad = grad.astype(F32)
    total = jnp.sum(grad * grad)
    return (grad / (jnp.sqrt(total) + 1e-07)).astype(BF)


def polynomial(gram, square):
    return (coef_b * gram.astype(F32) + coef_c * square).astype(BF)


def step(x):
    half = x.shape[0] // 2
    cat = jnp.concatenate
    gram = dot_nt(x, x).astype(BF)
    upper, lower = gram[:half], gram[half:]
    b01 = polynomial(upper[:, half:], dot(upper, gram[:, half:]))
    b10 = b01.T
    b00 = polynomial(upper[:, :half], dot(upper, gram[:, :half]))
    b11 = polynomial(lower[:, half:], dot(lower, gram[:, half:]))
    y0 = coef_a * x[:half].astype(F32) + dot(cat([b00, b01], 1), x)
    y1 = coef_a * x[half:].astype(F32) + dot(cat([b10, b11], 1), x)
    return cat([y0.astype(BF), y1.astype(BF)], 0)


def steps(x, count):
    for _ in range(count):
        x = step(x)
    return x


def updated(weight, x):
    step_size = 0.4 * math.sqrt(x.shape[-1])
    return (weight.astype(F32) - step_size * x.astype(F32)).astype(BF)


def first_steps_kernel(p0, p1, p2, p3, gate_hbm, gain_hbm, o_ref, gate, gain, whole, sems):
    made = copies([(gate_hbm, gate), (gain_hbm, gain)], sems)
    take_pieces((p0, p1, p2, p3), whole, PLANS["A"])
    o_ref[...] = steps(normalized(whole[...]), FIRST_STEPS)
    for copy in made:
        copy.wait()


def first_update_kernel(x_ref, w_hbm, o_ref, w, sems):
    (cw,) = copies([(w_hbm.at[0, 2], w)], sems)
    x = steps(x_ref[...], NS_STEPS - FIRST_STEPS)
    cw.wait()
    o_ref[...] = updated(w[...], x)


def core():
    return lax.axis_index("ctx") & 1


def pair_update_kernel(p0, p2, p1, p3, w_hbm, two, o_ref, o_hbm, w, whole, sems):
    cw, c2 = copies([(w_hbm.at[0, core()], w), (two, o_hbm.at[0, 2])], sems)
    pieces = (p0, p1, p2, p3)

    @pl.when(core() == 0)
    def _():
        take_pieces(pieces, whole, PLANS["B"])

    @pl.when(core() == 1)
    def _():
        take_pieces(pieces, whole, PLANS["C"])

    x = steps(normalized(whole[...]), NS_STEPS)
    cw.wait()
    o_ref[...] = updated(w[...], x)
    c2.wait()


def last_kernel(theirs, partial, o_hbm, sems):
    del partial
    (copy,) = copies([(theirs, o_hbm.at[0, 1 - core()])], sems)
    copy.wait()


def read_kernel(heads, w_hbm, *refs):
    queries, reads, (w1, w3, w2, sems) = refs[:heads], refs[heads : 2 * heads], refs[2 * heads :]
    c1, c3, c2 = copies([(w_hbm.at[0, i], w) for i, w in enumerate((w1, w3, w2))], sems)
    scale = w1.shape[-1] ** (-0.5)
    c1.wait()
    r1 = [dot(q[...], w1[...]) * scale for q in queries]
    c3.wait()
    r3 = [dot(q[...], w3[...]) * scale for q in queries]
    hq = [(a * jax.nn.sigmoid(a) * b).astype(BF) for a, b in zip(r1, r3)]
    c2.wait()
    for h, out in zip(hq, reads):
        out[...] = (dot(h, w2[...]) * scale).astype(BF)


def norm_kernel(heads, gate, gain, mine, partial, *refs):
    del partial
    reads, (out, o_hbm, sems) = refs[:heads], refs[heads:]
    made = copies([(mine, o_hbm.at[0, core()])], sems)
    width = reads[0].shape[-1]
    me = lax.axis_index("head")
    for r, read in enumerate(reads):
        at = pl.multiple_of(lax.rem(me + r, heads) * width, width)
        x = read[...].astype(F32)
        mean = jnp.mean(x * x, axis=-1, keepdims=True)
        g = gate[:, pl.ds(at, width)].astype(F32)
        out[:, pl.ds(at, width)] = (
            x * lax.rsqrt(mean + 1e-06) * gain[:, pl.ds(at, width)] * (g * jax.nn.sigmoid(g))
        ).astype(BF)
    for copy in made:
        copy.wait()


def local(ctx, heads, keys, values, rates, queries, fast_weights, gate, gain):
    tok, width = keys.shape
    bits = range(ctx.bit_length() - 1)
    halves = jax.ShapeDtypeStruct((width // 2, width), BF)
    matrix = jax.ShapeDtypeStruct((width, width), BF)
    mat = lambda dtype: pltpu.VMEM((width, width), dtype)
    tokens = lambda dtype: pltpu.VMEM((tok, width), dtype)
    sems = lambda n: pltpu.SemaphoreType.DMA((n,))

    hbm = lambda x: pltpu.with_memory_space_constraint(x, pltpu.HBM)

    def call(kernel, mib, **kw):
        def run(*args):
            return pl.pallas_call(
                kernel, compiler_params=pltpu.CompilerParams(vmem_limit_bytes=mib * MIB), **kw
            )(*args)

        return run

    def swap(x, bit):
        return lax.ppermute(x, "ctx", [(i, i ^ (1 << bit)) for i in range(ctx)])

    def turn(x, r):
        return lax.ppermute(x, "head", [(i, (i + r) % heads) for i in range(heads)])

    outs = call(
        functools.partial(grad_two_kernel, heads), 14,
        out_shape=[halves] * 2
        + [jax.ShapeDtypeStruct((tok, width), d) for d in (F32, F32, BF)]
        + [jax.ShapeDtypeStruct((tok, width), BF)]
        + [matrix]
        + [jax.ShapeDtypeStruct((queries.shape[0], width), BF)] * heads,
        in_specs=[HBM] * 5,
        out_specs=[VM] * (7 + heads),
        scratch_shapes=[tokens(BF), pltpu.VMEM(rates.shape, F32), mat(BF), mat(BF), mat(BF), sems(6 + heads)],
    )(hbm(keys), hbm(values), hbm(rates), hbm(fast_weights), hbm(queries))
    two, (g1, g3, go), (k, w2), columns = outs[:2], outs[2:5], outs[5:7], outs[7:]
    asked = [columns[0]] + [turn(columns[r], r) for r in range(1, heads)]
    outs = call(
        grad_one_kernel, 12,
        out_shape=[halves] * 4,
        in_specs=[VM] * 5,
        out_specs=[VM] * 4,
        scratch_shapes=[tokens(BF), tokens(BF), mat(BF)],
    )(k, w2, g1, g3, go)
    one, three = outs[:2], outs[2:]

    def add(x, y):
        return (x.astype(F32) + y.astype(F32)).astype(BF)

    def summed(n, p):
        plan = PLANS[n]
        keep, send = p
        got = swap(send, 0)
        quarter = width // 4

        give = add(keep[quarter:], got[quarter:])
        total, got = add(keep[:quarter], got[:quarter]), swap(give, plan[1])
        if len(plan) == 3:
            half = quarter // 2
            give = add(total[half:], got[half:])
            total, got = add(total[:half], got[:half]), swap(give, plan[2])
        for bit in bits:
            if bit not in plan:
                total = add(total, got)
                got = swap(total, bit)
        if len(plan) == 3:
            total = add(total, got)
            got = swap(total, plan[2])
            total = jnp.concatenate([total, got])
        else:
            total = add(total, got)
        return total, swap(total, plan[1])

    two, one, three = summed("A", two), summed("B", one), summed("C", three)

    def gathered(own):
        other = [swap(x, 0) for x in own]
        return own[0], other[0], own[1], other[1]

    gains = gain.reshape(1, -1)
    x_two, gate_here, gain_here = call(
        first_steps_kernel, 10,
        out_shape=[matrix] + [jax.ShapeDtypeStruct(x.shape, x.dtype) for x in (gate, gains)],
        in_specs=[VM] * 4 + [HBM] * 2,
        out_specs=[VM] * 3,
        scratch_shapes=[mat(BF), sems(2)],
    )(*gathered(two), hbm(gate), hbm(gains))
    new_two = call(
        first_update_kernel, 10,
        out_shape=matrix,
        in_specs=[VM, HBM],
        out_specs=VM,
        scratch_shapes=[mat(BF), sems(1)],
    )(x_two, hbm(fast_weights))
    keep, got = [], []
    for b, c in zip(one, three):
        keep.append(jnp.where(core() == 0, b, c))
        give = lax.select_n(jnp.broadcast_to(core() == 0, b.shape), b, c)
        got.append(swap(give, 0))
    mine, new_weights = call(
        pair_update_kernel, 10,
        out_shape=[matrix, jax.ShapeDtypeStruct(fast_weights.shape, BF)],
        in_specs=[VM] * 4 + [HBM, VM],
        out_specs=[VM, HBM],
        scratch_shapes=[mat(BF), mat(BF), sems(2)],
    )(*keep, *got, hbm(fast_weights), new_two)
    theirs = swap(mine, 0)

    reads = call(
        functools.partial(read_kernel, heads), 12,
        out_shape=[jax.ShapeDtypeStruct(x.shape, BF) for x in asked],
        in_specs=[HBM] + [VM] * heads,
        out_specs=[VM] * heads,
        scratch_shapes=[mat(BF)] * 3 + [sems(3)],
    )(hbm(fast_weights), *asked)
    back = [reads[0]] + [turn(reads[r], heads - r) for r in range(1, heads)]
    layer_out, new_weights = call(
        functools.partial(norm_kernel, heads), 8,
        out_shape=[
            jax.ShapeDtypeStruct(queries.shape, BF),
            jax.ShapeDtypeStruct(fast_weights.shape, BF),
        ],
        in_specs=[VM] * 3 + [HBM] + [VM] * heads,
        out_specs=[VM, HBM],
        scratch_shapes=[sems(1)],
        input_output_aliases={3: 1},
    )(gate_here, gain_here, mine, new_weights, *back)
    new_weights = call(
        last_kernel, 4,
        out_shape=jax.ShapeDtypeStruct(fast_weights.shape, BF),
        in_specs=[VM, HBM],
        out_specs=HBM,
        scratch_shapes=[sems(1)],
        input_output_aliases={1: 0},
    )(theirs, new_weights)
    return layer_out, new_weights


def solution(mesh):
    in_specs = (
        P("ctx", "head"),
        P("ctx", "head"),
        P("head", "ctx"),
        P(("ctx", "head"), None),
        P("head", None, None, None),
        P(("ctx", "head"), None),
        P(),
    )
    out_specs = (P(("ctx", "head"), None), P("head", None, None, None))

    def body(*args):
        return local(mesh.shape["ctx"], mesh.shape["head"], *args)

    return jax.shard_map(
        body, mesh=mesh, in_specs=in_specs, out_specs=out_specs, check_vma=False
    )
```
